512 devices in a mesh: tile: 32 (over y, x, core), depth: 16 (over z).
Axes of the slice: x: 4, y: 4, z: 16, core: 2. Of those that a mesh axis runs over, the one named last changes fastest.
Arguments:
- features: bfloat16 [16, 8192, 128], P('depth', 'tile'), may hold values from -4 to 4
- logits: float32 [16, 8192], P('depth', 'tile'), may hold values from -2.75 to 5.5
- geometry: float32 [2, 16, 5, 8192], P(None, 'depth', None, 'tile'), may hold values from -0.6 to 32, as said below
- dest_slot: int32 [2, 16, 8192], P(None, 'depth', 'tile'), may hold values from -1 to 8191, as said below
- target: bfloat16 [2, 64, 128, 1024], P(None, 'tile'), may hold values from -3 to 3
Outputs:
- images: bfloat16 [2, 64, 128, 1024], P(None, 'tile', None, 'depth')
- new_features: bfloat16 [16, 8192, 128], P('depth', 'tile')
- new_logits: float32 [16, 8192], P('depth', 'tile')
- shape_grads: float32 [2, 16, 5, 8192], P(None, 'depth', None, 'tile')
The draws below stay inside these ranges and needn't reach their ends.
Inputs may be any that keep to these rules, and one draw needn't show every extreme that they name: `dest_slot`: for each view and layer no two splats share a slot; -1 marks a splat outside the view; a splat's place within its tile is its front-to-back order. At most 8 splats of one layer held by one index of tile go to the tiles of one index of tile, and in every view and layer there is an index of tile whose tiles receive exactly 8 from every owner, so that all their slots are used. `geometry`: components 0 and 1 are a splat's centre in pixels within its tile, from 0 to 32; components 2 and 3 lie in -0.5 to 2.0; component 4 in -0.6 to 0.6.
All inputs are finite; a program needn't handle non-finite values.
Results may differ from the reference program's by a relative error of at most 0.0073.
Values may be sent and summed in bfloat16 or wider, within the bound.
No kernel may reach another device: no remote copies, remote signals or barrier semaphores. Data moves between devices by JAX's collectives and lax.ppermute only.
A program may use at most 64 MiB of HBM per device.

```python
import jax
import jax.numpy as jnp
from jax import lax

F = 128
W = 32
S = 128
VIEWS = 2
P_SIZE = 1024
LAYERS = 16
TILES = 64
OWN = 256
SPLATS = 8192
CAP = 8
N_TILE = 32


def draw_logits(key, part):
    key_base, key_flag, key_high = jax.random.split(jax.random.fold_in(key, 11), 3)
    base_draw = jax.random.uniform(key_base, (LAYERS, SPLATS), jnp.float32)
    flag_draw = jax.random.uniform(key_flag, (LAYERS, SPLATS), jnp.float32)
    high_draw = jax.random.uniform(key_high, (LAYERS, SPLATS), jnp.float32)
    high = 5.0 + 0.5 * high_draw
    low = -2.75 + 1.6 * base_draw
    opaque = flag_draw < 1.0 / 32.0
    return jnp.where(opaque, high, low)


def draw_geometry(key, part):
    key_mean, key_scale, key_corr = jax.random.split(jax.random.fold_in(key, 23), 3)
    means = jax.random.uniform(key_mean, (VIEWS, LAYERS, 2, SPLATS), jnp.float32) * W
    scale_draw = jax.random.uniform(key_scale, (VIEWS, LAYERS, 2, SPLATS), jnp.float32)
    corr_draw = jax.random.uniform(key_corr, (VIEWS, LAYERS, 1, SPLATS), jnp.float32)
    scales = -0.5 + 2.5 * scale_draw
    corr = 0.6 * (2.0 * corr_draw - 1.0)
    return jnp.concatenate([means, scales, corr], axis=2)


def one_layer_slots(layer_key):
    key_counts, key_hot, key_owner, key_recv = jax.random.split(layer_key, 4)
    counts = jax.random.randint(key_counts, (N_TILE, N_TILE), 1, CAP + 1)
    hottest = jax.random.randint(key_hot, (), 0, N_TILE)
    counts = jnp.where(jnp.arange(N_TILE)[None, :] == hottest, CAP, counts).astype(jnp.int32)
    ends = jnp.cumsum(counts, axis=1)
    starts = ends - counts
    arrivals = jnp.cumsum(counts, axis=0) - counts
    recv_table = jax.vmap(lambda table_key: jax.random.permutation(table_key, OWN))(jax.random.split(key_recv, N_TILE))
    positions = jnp.arange(OWN, dtype=jnp.int32)

    def owner_row(owner, owner_key):
        receiver = jnp.sum((positions[:, None] >= ends[owner][None, :]).astype(jnp.int32), axis=1)
        visible = receiver < N_TILE
        safe = jnp.minimum(receiver, N_TILE - 1)
        place_in = positions - starts[owner][safe]
        arrival = jnp.clip(arrivals[owner][safe] + place_in, 0, OWN - 1)
        local_slot = recv_table[safe, arrival]
        value = jnp.where(visible, safe * OWN + local_slot, -1).astype(jnp.int32)
        shuffle = jax.random.permutation(owner_key, OWN)
        return jnp.zeros((OWN,), jnp.int32).at[shuffle].set(value)
    rows = jax.vmap(owner_row)(jnp.arange(N_TILE, dtype=jnp.int32), jax.random.split(key_owner, N_TILE))
    return rows.reshape(SPLATS)


def draw_dest_slot(key, part):
    layer_keys = jax.random.split(jax.random.fold_in(key, 37), VIEWS * LAYERS)
    slots = jax.vmap(one_layer_slots)(layer_keys)
    return slots.reshape(VIEWS, LAYERS, SPLATS)


def shard_levels(rng, dims, cuts, low, largest):
    def one(position, blocks):
        heights = jax.random.uniform(jax.random.fold_in(jax.random.fold_in(rng, 6), position), (blocks,), jnp.float32, low / len(cuts), largest / len(cuts))
        return jnp.repeat(jnp.exp(heights), dims[position] // blocks).reshape((-1,) + (1,) * (len(dims) - position - 1))

    loudness = one(*cuts[0])
    for cut in cuts[1:]:
        loudness = loudness * one(*cut)
    return loudness


def centred(rng, extent, scale, most, shards=(), kind=jnp.bfloat16):
    entries = scale * jax.random.normal(rng, extent, jnp.float32)
    if shards:
        entries = entries * shard_levels(rng, extent, shards, -0.22, 0.18)
    return jnp.clip(entries, -most, most).astype(kind)


def setup_inputs(seed: int = 0) -> dict:
    arg_keys = jax.random.split(jax.random.key(seed), 6)
    return {
        "features": centred(arg_keys[0], (LAYERS, SPLATS, F), 1.0, 4.0, ((0, 16), (1, 32))),
        "logits": draw_logits(jax.random.fold_in(arg_keys[5], 71), 0),
        "geometry": draw_geometry(jax.random.fold_in(arg_keys[5], 71), 0),
        "dest_slot": draw_dest_slot(jax.random.fold_in(arg_keys[5], 71), 0),
        "target": centred(arg_keys[4], (VIEWS, TILES, F, P_SIZE), 0.5, 3.0, ((1, 32),)),
    }


clamp_top = 0.99
feature_rate = 0.5
opacity_rate = 0.5


def pixel_places():
    places = jnp.arange(P_SIZE, dtype=jnp.int32)
    across = (places % W).astype(jnp.float32) + 0.5
    downward = (places // W).astype(jnp.float32) + 0.5
    return across, downward


def splat_fields(shapes):
    across, downward = pixel_places()
    delta_x = across[None, :] - shapes[0][:, None]
    delta_y = downward[None, :] - shapes[1][:, None]
    coef_a = jnp.exp(shapes[2])[:, None]
    coef_c = jnp.exp(shapes[3])[:, None]
    spread = jnp.exp(0.5 * (shapes[2] + shapes[3]))[:, None]
    coef_b = shapes[4][:, None] * spread
    quadric = coef_a * delta_x * delta_x + 2.0 * coef_b * delta_x * delta_y + coef_c * delta_y * delta_y
    falloff = jnp.exp(-0.5 * quadric)
    opacity = shapes[5][:, None]
    product = opacity * falloff
    coverage = jnp.minimum(product, clamp_top)
    return delta_x, delta_y, coef_a, coef_b, coef_c, spread, falloff, opacity, product, coverage


def layer_forward(inputs):
    slot_feats, shapes = inputs
    coverage = splat_fields(shapes)[9]
    log_keep = jnp.log(1.0 - coverage)
    before = jnp.cumsum(log_keep, axis=0) - log_keep
    weights = (coverage * jnp.exp(before)).astype(jnp.bfloat16)
    composite = jnp.dot(slot_feats.T, weights, preferred_element_type=jnp.float32)
    layer_keep = jnp.exp(jnp.sum(log_keep, axis=0))
    return composite, layer_keep


def layer_backward(inputs):
    slot_feats, shapes, grad_comp, grad_keep = inputs
    delta_x, delta_y, coef_a, coef_b, coef_c, spread, falloff, opacity, product, coverage = splat_fields(shapes)
    log_keep = jnp.log(1.0 - coverage)
    before = jnp.cumsum(log_keep, axis=0) - log_keep
    decayed = jnp.exp(before)
    exact_weight = coverage * decayed
    weights = exact_weight.astype(jnp.bfloat16)
    layer_keep = jnp.exp(jnp.sum(log_keep, axis=0))
    grad_feat = jnp.dot(weights, grad_comp.T, preferred_element_type=jnp.float32)
    grad_weight = jnp.dot(slot_feats, grad_comp, preferred_element_type=jnp.float32)
    grad_before = grad_weight * exact_weight
    later = jnp.sum(grad_before, axis=0)[None, :] - jnp.cumsum(grad_before, axis=0)
    grad_log = later + (grad_keep * layer_keep)[None, :]
    grad_coverage = grad_weight * decayed - grad_log / (1.0 - coverage)
    grad_product = jnp.where(product < clamp_top, grad_coverage, 0.0)
    grad_quadric = -0.5 * opacity * falloff * grad_product
    grad_mean_x = -2.0 * jnp.sum(grad_quadric * (coef_a * delta_x + coef_b * delta_y), axis=1)
    grad_mean_y = -2.0 * jnp.sum(grad_quadric * (coef_b * delta_x + coef_c * delta_y), axis=1)
    grad_first = jnp.sum(grad_quadric * delta_x * delta_x, axis=1)
    grad_cross = jnp.sum(grad_quadric * 2.0 * delta_x * delta_y, axis=1)
    grad_second = jnp.sum(grad_quadric * delta_y * delta_y, axis=1)
    grad_log_a = coef_a[:, 0] * grad_first + 0.5 * coef_b[:, 0] * grad_cross
    grad_log_c = coef_c[:, 0] * grad_second + 0.5 * coef_b[:, 0] * grad_cross
    grad_corr = spread[:, 0] * grad_cross
    opacity_flat = opacity[:, 0]
    grad_logit = opacity_flat * (1.0 - opacity_flat) * jnp.sum(falloff * grad_product, axis=1)
    grad_shape = jnp.stack([grad_mean_x, grad_mean_y, grad_log_a, grad_log_c, grad_corr, grad_logit])
    return grad_feat, grad_shape


def pick_rows(source_rows, chosen):
    return source_rows[chosen]


def pick_columns(source_rows, chosen):
    return source_rows[:, chosen]


def reference(features, logits, geometry, dest_slot, target):
    slot_total = TILES * S
    splat_feats = features
    logit_now = logits
    images = []
    shape_grads = []
    splat_ids = jnp.arange(SPLATS, dtype=jnp.int32)
    for view_index in range(VIEWS):
        slot_ids = dest_slot[view_index]
        holder = jnp.where(slot_ids >= 0, slot_ids, slot_total).astype(jnp.int32)
        owner_of = jax.vmap(lambda target_row: jnp.full((slot_total,), -1, jnp.int32).at[target_row].set(splat_ids, mode="drop"))(holder)
        filled = owner_of >= 0
        picks = jnp.maximum(owner_of, 0).astype(jnp.int32)
        slot_feats = jax.vmap(pick_rows)(splat_feats, picks)
        slot_feats = jnp.where(filled[:, :, None], slot_feats, jnp.zeros_like(slot_feats))
        opacity = jax.nn.sigmoid(logit_now)
        shape_source = jnp.concatenate([geometry[view_index], opacity[:, None, :]], axis=1)
        slot_shapes = jax.vmap(pick_columns)(shape_source, picks)
        slot_shapes = jnp.where(filled[:, None, :], slot_shapes, jnp.zeros_like(slot_shapes))
        tile_feats = slot_feats.reshape(LAYERS * TILES, S, F)
        tile_shapes = slot_shapes.reshape(LAYERS, 6, TILES, S).transpose(0, 2, 1, 3).reshape(LAYERS * TILES, 6, S)
        composites, layer_keeps = lax.map(layer_forward, (tile_feats, tile_shapes))
        composites = composites.reshape(LAYERS, TILES, F, P_SIZE)
        layer_keeps = layer_keeps.reshape(LAYERS, TILES, P_SIZE)
        ahead = jnp.concatenate([jnp.ones((1, TILES, P_SIZE), jnp.float32), jnp.cumprod(layer_keeps, axis=0)[:-1]], axis=0)
        summed = jnp.sum(ahead[:, :, None, :] * composites, axis=0)
        images.append(summed.astype(jnp.bfloat16))
        residual = summed - target[view_index].astype(jnp.float32)
        pixel_terms = jnp.sum(residual[None] * composites, axis=2)

        def rear_step(carried, pair):
            keep_here, term_here = pair
            return term_here + keep_here * carried, carried

        _, behind_flipped = lax.scan(rear_step, jnp.zeros((TILES, P_SIZE), jnp.float32), (layer_keeps[::-1], pixel_terms[::-1]))
        behind = behind_flipped[::-1]
        grad_keep = ahead * behind
        grad_comp = (ahead[:, :, None, :] * residual[None]).astype(jnp.bfloat16)
        grad_feat, grad_shape = lax.map(layer_backward, (tile_feats, tile_shapes, grad_comp.reshape(LAYERS * TILES, F, P_SIZE), grad_keep.reshape(LAYERS * TILES, P_SIZE)))
        grad_feat = grad_feat.reshape(LAYERS, slot_total, F)
        grad_shape = grad_shape.reshape(LAYERS, TILES, 6, S).transpose(0, 2, 1, 3).reshape(LAYERS, 6, slot_total)
        visible = slot_ids >= 0
        fetched = jnp.where(visible, slot_ids, 0).astype(jnp.int32)
        splat_grad_feat = jax.vmap(pick_rows)(grad_feat, fetched)
        splat_grad_feat = jnp.where(visible[:, :, None], splat_grad_feat, jnp.zeros_like(splat_grad_feat))
        splat_grad_shape = jax.vmap(pick_columns)(grad_shape, fetched)
        splat_grad_shape = jnp.where(visible[:, None, :], splat_grad_shape, jnp.zeros_like(splat_grad_shape))
        shape_grads.append(splat_grad_shape[:, :5])
        splat_feats = (splat_feats.astype(jnp.float32) - feature_rate * splat_grad_feat).astype(jnp.bfloat16)
        logit_now = logit_now - opacity_rate * splat_grad_shape[:, 5]
    return jnp.stack(images), splat_feats, logit_now, jnp.stack(shape_grads)
```

```python
import math
from functools import partial

import jax
import jax.numpy as jnp
from jax import lax
from jax.experimental import pallas as pl
from jax.experimental.pallas import tpu as pltpu
from jax.sharding import Mesh, PartitionSpec as P

F = 128
W = 32
S = 128
VIEWS = 2
P_SIZE = 1024
SHARE = 64
CAP = 8
ROWS = F + 8
GROUP = 1
UNROLL = 2
VMEM_LIMIT = 16 << 20

CLAMP = 0.99
RATE = 0.5
LOG2E = math.log2(math.e)

BF = jnp.bfloat16
F32 = jnp.float32
VMEM = pl.BlockSpec(memory_space=pltpu.VMEM)
SMEM = pl.BlockSpec(memory_space=pltpu.SMEM)


def dot(a, b, ca, cb):
    return lax.dot_general(a, b, (((ca,), (cb,)), ((), ())), preferred_element_type=F32)


def iota(shape, dim):
    return lax.broadcasted_iota(jnp.int32, shape, dim)


def split3(x):
    hi = x.astype(BF).astype(F32)
    rest = x - hi
    mid = rest.astype(BF).astype(F32)
    return hi, mid, rest - mid


def split2(x):
    hi = x.astype(BF)
    return hi, (x - hi.astype(F32)).astype(BF)


def joined3(x):
    return x[0:8] + (x[8:16] + x[16:24])


def stacked3(rows):
    hi, mid, lo = split3(rows)
    blank = jnp.zeros((F - 24, rows.shape[1]), F32)
    return jnp.concatenate([hi, mid, lo, blank], axis=0).astype(BF)


def strict(n, lower):
    i, j = iota((n, n), 0), iota((n, n), 1)
    return jnp.where(i > j if lower else i < j, 1.0, 0.0).astype(BF)


def routes(slots):
    owned = slots.shape[1]
    owners = owned // CAP
    visible = slots >= 0
    receiver = jnp.where(visible, slots >> (owned.bit_length() - 1), -1)
    to = jnp.where(receiver == iota((owners, owned), 0), 1.0, 0.0)
    rank = dot(to.astype(BF), strict(owned, False), 1, 0)
    place = jnp.sum(to * rank, axis=0, keepdims=True).astype(jnp.int32)
    position = jnp.where(visible, receiver * CAP + place, -1)
    return jnp.where(position == iota((owned, owned), 0), 1.0, 0.0).astype(BF)


def pack(feats, logits, slots, hot, row_ref, out_ref):
    owned = slots.shape[1]
    row_ref[5:6, :] = 1.0 / (1.0 + jnp.exp(-logits))
    row_ref[6:7, :] = ((slots & (owned - 1)) + 1).astype(F32)
    rows = dot(hot, feats, 1, 0).astype(BF)
    extra = dot(hot, stacked3(row_ref[...]), 1, 1).astype(BF)
    for copy in range(out_ref.shape[0] // owned):
        out_ref[copy * owned : (copy + 1) * owned, 0:F] = rows
        out_ref[copy * owned : (copy + 1) * owned, F : 2 * F] = extra


def route_kernel(slots_ref, hot_ref, *, view):
    hot_ref[...] = routes(slots_ref[view])


def geometry_rows(geometry_ref, row_ref, view):
    row_ref[...] = jnp.zeros_like(row_ref)
    for k in range(5):
        row_ref[k : k + 1, :] = geometry_ref[view * 5 + k]


def pack_kernel(feats_ref, logits_ref, geometry_ref, slots_ref, out_ref, hot_ref, row_ref):
    slots = slots_ref[0]
    hot = routes(slots)
    hot_ref[...] = hot
    geometry_rows(geometry_ref, row_ref, 0)
    pack(feats_ref[...], logits_ref[...], slots, hot, row_ref, out_ref)


def update(ret_ref, feats_ref, logits_ref, hot):
    owned = hot.shape[0]
    total = jnp.zeros((owned, F), F32)
    extra = jnp.zeros((8, owned), F32)
    for copy in range(ret_ref.shape[0] // owned):
        block = slice(copy * owned, (copy + 1) * owned)
        total += dot(hot, ret_ref[block, 0:F], 0, 0)
        total += dot(hot, ret_ref[block, F : 2 * F], 0, 0)
        extra += joined3(dot(ret_ref[block, 2 * F : 3 * F], hot, 0, 0))
    feats = (feats_ref[...].astype(F32) - RATE * total).astype(BF)
    logits = logits_ref[...] - RATE * extra[5:6]
    return feats, logits, extra


def update_pack_kernel(
    ret_ref,
    feats_ref,
    logits_ref,
    slots_ref,
    geometry_ref,
    hot_ref,
    next_ref,
    out_ref,
    new_feats_ref,
    new_logits_ref,
    grads_ref,
    row_ref,
    *,
    view,
):
    feats, logits, extra = update(ret_ref, feats_ref, logits_ref, hot_ref[...])
    grads_ref[...] = extra
    new_feats_ref[...] = feats
    new_logits_ref[...] = logits
    geometry_rows(geometry_ref, row_ref, view)
    pack(feats, logits, slots_ref[view], next_ref[...], row_ref, out_ref)


def update_kernel(
    ret_ref,
    feats_ref,
    logits_ref,
    hot_ref,
    *refs,
):
    *earlier, new_feats_ref, new_logits_ref, grads_ref = refs
    feats, logits, extra = update(ret_ref, feats_ref, logits_ref, hot_ref[...])
    new_feats_ref[...] = feats
    new_logits_ref[...] = logits
    for v, rows in enumerate([ref[...] for ref in earlier] + [extra]):
        for k in range(5):
            grads_ref[v * 5 + k] = rows[k : k + 1]


def landing(got_ref, layer, owned):
    block = slice(layer * owned, (layer + 1) * owned)
    slot = got_ref[block, F : 2 * F].astype(F32)[:, 6:7]
    lane = (iota((owned, owned), 1) + 1).astype(F32)
    return jnp.where(slot == lane, 1.0, 0.0).astype(BF)


def columns(shapes_ref, tile, width):
    cols = slice(tile * width, (tile + 1) * width)
    g0 = shapes_ref[0:1, cols]
    g2, g3 = shapes_ref[2:3, cols], shapes_ref[3:4, cols]
    coef_a, coef_c = jnp.exp(g2), jnp.exp(g3)
    spread = jnp.exp(0.5 * (g2 + g3))
    coef_b = shapes_ref[4:5, cols] * spread
    delta_x = iota((W, width), 0).astype(F32) + 0.5 - g0
    return coef_a, coef_b, coef_c, spread, delta_x


def x_terms(shapes_ref, x_ref, width):
    for tile in range(2):
        coef_a, coef_b, coef_c, _, delta_x = columns(shapes_ref, tile, width)
        x_ref[0, tile] = (-0.5 * LOG2E) * coef_a * delta_x * delta_x
        x_ref[1, tile] = (-LOG2E) * coef_b * delta_x
        x_ref[2, tile] = delta_x
        x_ref[3, tile, 0:1] = (-0.5 * LOG2E) * coef_c


def products(shapes_ref, x_ref, top, width):
    parts = []
    for tile in range(2):
        cols = slice(tile * width, (tile + 1) * width)
        for line in range(SHARE // W):
            delta_y = (top + (line + 0.5)) - shapes_ref[1:2, cols]
            level = x_ref[3, tile, 0:1] * delta_y * delta_y
            power = x_ref[0, tile] + (x_ref[1, tile] * delta_y + level)
            parts.append(jnp.exp2(power) * shapes_ref[5:6, cols])
    return jnp.concatenate(parts, axis=0)


def apart(weights, width):
    half = weights.shape[0] // 2
    blank = jnp.zeros((half, width), BF)
    return jnp.concatenate(
        [
            jnp.concatenate([weights[:half], blank], axis=1),
            jnp.concatenate([blank, weights[half:]], axis=1),
        ],
        axis=0,
    )


def parts_rows(rows):
    hi, mid, lo = split3(rows)
    k = iota(rows.shape, 0)
    return jnp.where(
        k == 0, hi, jnp.where(k == 1, mid, jnp.where(k == 2, lo, 0.0))
    ).astype(BF)


def share_top(pos_ref, chunk, group):
    return ((SHARE // W) * (chunk * group + pos_ref[0])).astype(F32)


def forward_kernel(
    pos_ref, got_ref, out_ref, feats_ref, shapes_ref, hot_ref, x_ref, tri_ref
):
    owned = 2 * S
    group = got_ref.shape[0] // owned
    width = S * group
    for layer in range(group):
        block = slice(layer * owned, (layer + 1) * owned)
        hot = landing(got_ref, layer, owned)
        hot_ref[block, :] = hot
        feats = dot(got_ref[block, 0:F], hot, 0, 0).astype(BF)
        shapes = joined3(dot(got_ref[block, F : 2 * F], hot, 0, 0))
        for tile in range(2):
            at = slice(tile * width + layer * S, tile * width + (layer + 1) * S)
            feats_ref[:, at] = feats[:, tile * S : (tile + 1) * S]
            shapes_ref[:, at] = shapes[:, tile * S : (tile + 1) * S]
    x_terms(shapes_ref, x_ref, width)
    tri_ref[0:width, :] = strict(width, False)
    tri_ref[width : 2 * width, :] = tri_ref[0:width, :]
    ones = jnp.ones((8, 2 * width), BF)

    def step(chunk, carry):
        product = products(shapes_ref, x_ref, share_top(pos_ref, chunk, group), width)
        coverage = jnp.minimum(product, CLAMP)
        pieces = jnp.concatenate(split2(jnp.log(1.0 - coverage)), axis=1)
        before = dot(pieces, tri_ref[...], 1, 0)
        weights = (coverage * jnp.exp(before)).astype(BF)
        out_ref[chunk, 0:F, :] = dot(feats_ref[...], apart(weights, width), 1, 1).astype(BF)
        out_ref[chunk, F:ROWS, :] = parts_rows(jnp.exp(dot(ones, pieces, 1, 1)))
        return carry

    lax.fori_loop(0, out_ref.shape[0], step, 0, unroll=UNROLL)


def prepare_kernel(pos_ref, shapes_ref, exact_ref, odds_ref, x_ref, tri_ref):
    width = exact_ref.shape[2]
    group = width // S
    x_terms(shapes_ref, x_ref, width)
    tri_ref[0:width, :] = strict(width, False)
    tri_ref[width : 2 * width, :] = tri_ref[0:width, :]

    def step(chunk, carry):
        product = products(shapes_ref, x_ref, share_top(pos_ref, chunk, group), width)
        coverage = jnp.minimum(product, CLAMP)
        left = 1.0 - coverage
        before = dot(jnp.concatenate(split2(jnp.log(left)), axis=1), tri_ref[...], 1, 0)
        exact_ref[chunk] = coverage * jnp.exp(before)
        odds_ref[chunk] = jnp.where(product < CLAMP, product / left, 0.0)
        return carry

    lax.fori_loop(0, exact_ref.shape[0], step, 0, unroll=UNROLL)


def pixel_kernel(got_ref, target_ref, image_ref, out_ref):
    groups = got_ref.shape[0]
    summed = jnp.zeros((F, 2 * SHARE), F32)
    ahead = jnp.ones((1, 2 * SHARE), F32)
    aheads, keeps = [], []
    for d in range(groups):
        rows = got_ref[d, F:ROWS, :].astype(F32)
        keep = rows[0:1] + (rows[1:2] + rows[2:3])
        summed += ahead * got_ref[d, 0:F, :].astype(F32)
        aheads.append(ahead)
        keeps.append(keep)
        ahead = ahead * keep
    image_ref[...] = summed.T.astype(BF)
    residual = summed - target_ref[...].astype(F32)
    behind = jnp.zeros((1, 2 * SHARE), F32)
    for d in reversed(range(groups)):
        carry = aheads[d] * behind * keeps[d]
        out_ref[d, 0:F, :] = (aheads[d] * residual).astype(BF)
        out_ref[d, F:ROWS, :] = parts_rows(jnp.broadcast_to(carry, (8, 2 * SHARE)))
        if d:
            term = jnp.sum(residual * got_ref[d, 0:F, :].astype(F32), axis=0, keepdims=True)
            behind = term + keeps[d] * behind


def folded(x):
    total = x[0:8]
    for k in range(8, x.shape[0], 8):
        total = total + x[k : k + 8]
    return total


def backward_kernel(
    pos_ref,
    hot_ref,
    feats_ref,
    shapes_ref,
    exact_ref,
    odds_ref,
    grad_ref,
    out_ref,
    x_ref,
    tri_ref,
    sum_ref,
    acc_ref,
):
    owned = 2 * S
    group = hot_ref.shape[0] // owned
    width = S * group
    for tile in range(2):
        x_ref[tile] = columns(shapes_ref, tile, width)[4]
    tri_ref[0:width, :] = strict(width, True)
    tri_ref[width : 2 * width, :] = tri_ref[0:width, :]
    sum_ref[...] = jnp.zeros_like(sum_ref)
    acc_ref[...] = jnp.zeros_like(acc_ref)
    ones = jnp.ones((8, width), BF)

    def step(chunk, carry):
        exact = exact_ref[chunk]
        odds = odds_ref[chunk]
        grad = grad_ref[chunk, 0:F, :]
        both = dot(grad, feats_ref[...], 0, 0)
        grad_weight = jnp.concatenate(
            [both[0:SHARE, 0:width], both[SHARE : 2 * SHARE, width : 2 * width]], axis=0
        )
        grad_before = grad_weight * exact
        later = dot(jnp.concatenate(split2(grad_before), axis=1), tri_ref[...], 1, 0)
        grad_log = later + dot(grad_ref[chunk, F:ROWS, :], ones, 0, 0)
        acc_ref[...] += dot(grad, apart(exact.astype(BF), width), 1, 0)
        scaled = jnp.where(odds > 0.0, grad_before, 0.0) - grad_log * odds
        top = share_top(pos_ref, chunk, group)
        for tile in range(2):
            delta_x = x_ref[tile]
            g1 = shapes_ref[1:2, tile * width : (tile + 1) * width]
            for line in range(SHARE // W):
                k = tile * (SHARE // W) + line
                delta_y = (top + (line + 0.5)) - g1
                row = scaled[k * W : (k + 1) * W]
                row_x = row * delta_x
                sum_0, sum_x, sum_xx = folded(row), folded(row_x), folded(row_x * delta_x)
                sum_y = sum_0 * delta_y
                sum_ref[tile, 0] += sum_0
                sum_ref[tile, 1] += sum_x
                sum_ref[tile, 2] += sum_y
                sum_ref[tile, 3] += sum_xx
                sum_ref[tile, 4] += sum_x * delta_y
                sum_ref[tile, 5] += sum_y * delta_y
        return carry

    lax.fori_loop(0, grad_ref.shape[0], step, 0, unroll=UNROLL)
    for tile in range(2):
        cols = slice(tile * width, (tile + 1) * width)
        coef_a, coef_b, coef_c, spread, _ = columns(shapes_ref, tile, width)
        total = [jnp.sum(sum_ref[tile, k], axis=0, keepdims=True) for k in range(6)]
        first, cross, second = -0.5 * total[3], -total[4], -0.5 * total[5]
        sum_ref[tile, 0, 0:1] = coef_a * total[1] + coef_b * total[2]
        sum_ref[tile, 0, 1:2] = coef_b * total[1] + coef_c * total[2]
        sum_ref[tile, 0, 2:3] = coef_a * first + 0.5 * coef_b * cross
        sum_ref[tile, 0, 3:4] = coef_c * second + 0.5 * coef_b * cross
        sum_ref[tile, 0, 4:5] = spread * cross
        sum_ref[tile, 0, 5:6] = (1.0 - shapes_ref[5:6, cols]) * total[0]
        sum_ref[tile, 0, 6:8] = jnp.zeros((2, width), F32)
    for layer in range(group):
        block = slice(layer * owned, (layer + 1) * owned)
        hot = hot_ref[block, :]
        feat = jnp.concatenate(
            [acc_ref[:, t * width + layer * S : t * width + (layer + 1) * S] for t in range(2)],
            axis=1,
        )
        rows = jnp.concatenate(
            [sum_ref[t, 0, :, layer * S : (layer + 1) * S] for t in range(2)], axis=1
        )
        hi, lo = split2(feat)
        out_ref[block, 0:F] = dot(hot, hi, 1, 1).astype(BF)
        out_ref[block, F : 2 * F] = dot(hot, lo, 1, 1).astype(BF)
        out_ref[block, 2 * F : 3 * F] = dot(hot, stacked3(rows), 1, 1).astype(BF)


def call(kernel, outs, ins, scratch=(), name=None, cost=None):
    specs = [SMEM if x.dtype == jnp.int32 and x.shape == (1,) else VMEM for x in ins]
    return pl.pallas_call(
        kernel,
        out_shape=tuple(jax.ShapeDtypeStruct(shape, dtype) for shape, dtype in outs),
        in_specs=specs,
        out_specs=tuple(VMEM for _ in outs),
        scratch_shapes=list(scratch),
        compiler_params=pltpu.CompilerParams(vmem_limit_bytes=VMEM_LIMIT),
        cost_estimate=cost,
        name=name,
    )(*ins)


def exchanged(x, axis, size):
    blocks = x.reshape(size, x.shape[0] // size, *x.shape[1:])
    return lax.all_to_all(blocks, axis, split_axis=0, concat_axis=0, tiled=True).reshape(x.shape)


def body(features, logits, geometry, dest_slot, target):
    owners = lax.axis_size("tile")
    group = lax.axis_size("low")
    groups = lax.axis_size("high")
    low = lax.axis_index("low")
    depth_here = lax.axis_index("high") * group + low
    owned = features.shape[1]
    width = S * group
    pos = low.astype(jnp.int32).reshape(1)
    around = ("low", "tile") if group > 1 else "tile"
    feats, now = features[0], logits
    slots = dest_slot
    geometry = geometry.transpose(0, 2, 1, 3).reshape(VIEWS * 5, 1, owned)
    targets = [
        lax.dynamic_slice_in_dim(target[v], depth_here * SHARE, SHARE, 2)
        .transpose(1, 0, 2)
        .reshape(F, 2 * SHARE)
        for v in range(VIEWS)
    ]
    send_shape = ((group * owned, 2 * F), BF)
    hot_shape = ((owned, owned), BF)
    row_scratch = pltpu.VMEM((8, owned), F32)
    x_scratch = pltpu.VMEM((4, 2, W, width), F32)
    tri_scratch = pltpu.VMEM((2 * width, width), BF)
    plane = ((groups, 2 * SHARE, width), F32)
    send, hot = call(
        pack_kernel,
        [send_shape, hot_shape],
        [feats, now, geometry, slots],
        [row_scratch],
        "pack",
    )
    images, shape_grads = [], []
    for v in range(VIEWS):
        got = exchanged(send, around, group * owners)
        composites, slot_feats, slot_shapes, landed = call(
            forward_kernel,
            [
                ((groups, ROWS, 2 * SHARE), BF),
                ((F, 2 * width), BF),
                ((8, 2 * width), F32),
                ((group * owned, owned), BF),
            ],
            [pos, got],
            [x_scratch, tri_scratch],
            "forward",
        )
        arrived = exchanged(composites, "high", groups)
        exact, odds = call(
            prepare_kernel,
            [plane, plane],
            [pos, slot_shapes],
            [x_scratch, tri_scratch],
            "prepare",
        )
        image, grad_comp = call(
            pixel_kernel,
            [((2 * SHARE, F), BF), ((groups, ROWS, 2 * SHARE), BF)],
            [arrived, targets[v]],
            name="pixels",
        )
        images.append(image.reshape(2, SHARE, F))
        grads = exchanged(grad_comp, "high", groups)
        (back,) = call(
            backward_kernel,
            [((group * owned, 3 * F), BF)],
            [pos, landed, slot_feats, slot_shapes, exact, odds, grads],
            [
                pltpu.VMEM((2, W, width), F32),
                tri_scratch,
                pltpu.VMEM((2, 6, 8, width), F32),
                pltpu.VMEM((F, 2 * width), F32),
            ],
            "backward",
        )
        ret = exchanged(back, around, group * owners)
        state = [((owned, F), BF), ((1, owned), F32)]
        if v + 1 < VIEWS:
            (next_hot,) = call(
                partial(route_kernel, view=v + 1), [hot_shape], [slots], name="route"
            )
            send, feats, now, shape_grad = call(
                partial(update_pack_kernel, view=v + 1),
                [send_shape, *state, ((8, owned), F32)],
                [ret, feats, now, slots, geometry, hot, next_hot],
                [row_scratch],
                "update_pack",
            )
            shape_grads.append(shape_grad)
            hot = next_hot
        else:
            feats, now, grads = call(
                update_kernel,
                [*state, ((VIEWS * 5, 1, owned), F32)],
                [ret, feats, now, hot, *shape_grads],
                name="update",
            )
    grads = grads.reshape(VIEWS, 5, 1, owned).transpose(0, 2, 1, 3)
    return (jnp.stack(images).transpose(0, 1, 3, 2), feats[None], now, grads)


def solution(mesh):
    tiles, layers = mesh.devices.shape
    split = Mesh(
        mesh.devices.reshape(tiles, layers // GROUP, GROUP), ("tile", "high", "low")
    )
    depth = ("high", "low")
    return jax.shard_map(
        body,
        mesh=split,
        in_specs=(
            P(depth, "tile", None),
            P(depth, "tile"),
            P(None, depth, None, "tile"),
            P(None, depth, "tile"),
            P(None, "tile", None, None),
        ),
        out_specs=(
            P(None, "tile", None, depth),
            P(depth, "tile", None),
            P(depth, "tile"),
            P(None, depth, None, "tile"),
        ),
        check_vma=False,
    )
```
